512 devices in a mesh: leaf: 128 (over z, y, core), rhs: 4 (over x).
Axes of the slice: x: 4, y: 8, z: 8, core: 2. Of those that a mesh axis runs over, the one named last changes fastest.
Arguments:
- potential: float32 [128, 1048576], P('rhs', 'leaf'), may hold values from -6 to 6
- geometry: float32 [4, 1048576], P(None, 'leaf'), as said below
- near_count: int32 [4096], P('leaf'), may hold values from 3 to 12, as said below
- near_offset: int32 [4096, 12], P('leaf'), may hold values from -6 to 6, as said below
- far_offset: int32 [4096, 4], P('leaf'), may hold values from -8 to 8, as said below
- col_basis: bfloat16 [4096, 256, 64], P('leaf'), may hold values from -0.375 to 0.375
- row_basis: bfloat16 [4096, 256, 64], P('leaf'), may hold values from -0.5 to 0.5
- leaf_up: bfloat16 [4096, 64, 64], P('leaf'), may hold values from -0.125 to 0.125
- leaf_down: bfloat16 [4096, 64, 64], P('leaf'), may hold values from -0.75 to 0.75
- leaf_coupling: bfloat16 [4096, 4, 64, 64], P('leaf'), may hold values from -0.375 to 0.375
- up_transfer: bfloat16 [2, 64, 64], replicated, may hold values from -0.5 to 0.5
- down_transfer: bfloat16 [2, 64, 64], replicated, may hold values from -0.75 to 0.75
- sibling_coupling: bfloat16 [2, 64, 64], replicated, may hold values from -0.375 to 0.375
Outputs:
- field: float32 [128, 1048576], P('rhs', 'leaf')
The draws below stay inside these ranges and needn't reach their ends.
Inputs may be any that keep to these rules, and one draw needn't show every extreme that they name: `geometry`: rows 0 to 2 are panel centroids, row 3 panel areas between 0.005 and 0.05. Each leaf cluster uses slots 0 to near_count - 1; some cluster uses all 12. `near_offset`: slot 0 of every cluster is the cluster itself (offset 0), slot 1 holds a positive offset and slot 2 a negative one; the other slots of a cluster hold distinct nonzero offsets. `far_offset`: every offset has magnitude above 6; the offsets of one cluster are distinct.
All inputs are finite; a program needn't handle non-finite values.
Results may differ from the reference program's by a relative error of at most 0.007.
Values may be sent and summed in bfloat16 or wider, within the bound.
No kernel may reach another device: no remote copies, remote signals or barrier semaphores. Data moves between devices by JAX's collectives and lax.ppermute only.
A program may use at most 64 MiB of HBM per device.

```python
import math
import jax
import jax.numpy as jnp
from jax import lax

P_SIZE = 256
K = 64
NNEAR = 12
NF0 = 4
NWIN = 6
FWIN = 8
LC_DEV = 32
R = 128
NCL = 4096
PANELS = 1048576
LEVELS = 7
N_LEAF = 128


def draw_geometry(key, part=0):
    panel_total = NCL * P_SIZE
    cluster = jnp.arange(panel_total, dtype=jnp.int32) // P_SIZE
    grid_first = jnp.zeros((panel_total,), jnp.int32)
    grid_second = jnp.zeros((panel_total,), jnp.int32)
    grid_third = jnp.zeros((panel_total,), jnp.int32)
    for bit_level in range(10):
        scale_bits = 8 ** bit_level
        grid_first = grid_first + cluster // scale_bits % 2 * 2 ** bit_level
        grid_second = grid_second + cluster // (scale_bits * 2) % 2 * 2 ** bit_level
        grid_third = grid_third + cluster // (scale_bits * 4) % 2 * 2 ** bit_level
    centres = jnp.stack([grid_first, grid_second, grid_third]).astype(jnp.float32) * 0.25
    positions = centres + jax.random.uniform(jax.random.fold_in(key, 1), (3, panel_total), jnp.float32)
    panel_areas = jnp.exp(jax.random.uniform(jax.random.fold_in(key, 2), (1, panel_total), jnp.float32, math.log(0.005), math.log(0.05)))
    return jnp.concatenate([positions, panel_areas], axis=0)


def draw_near_count(key, part=0):
    device_level = jax.random.randint(jax.random.fold_in(key, 11), (NCL // LC_DEV,), 3, NNEAR + 1)
    per_cluster = jnp.repeat(device_level, LC_DEV)
    dropped = jax.random.randint(jax.random.fold_in(key, 12), (NCL,), 0, NNEAR) % (per_cluster // 2 + 1)
    counted = jnp.maximum(per_cluster - dropped, 3)
    chosen = jax.random.randint(jax.random.fold_in(key, 13), (), 0, NCL)
    return jnp.where(jnp.arange(NCL, dtype=jnp.int32) == chosen, NNEAR, counted).astype(jnp.int32)


def distinct_order(key, candidates, taken):
    numbers = jnp.arange(candidates, dtype=jnp.int32)
    scores = jax.random.randint(key, (NCL, candidates), 0, 2 ** 20) * candidates + numbers[None, :]
    forced = jnp.where(numbers == 0, -2, jnp.where(numbers == candidates - 1, -1, 0))
    first_row = (jnp.arange(NCL, dtype=jnp.int32) == 0)[:, None]
    scores = jnp.where(first_row & (forced[None, :] < 0), forced[None, :], scores)
    return jnp.argsort(scores, axis=1, stable=True)[:, :taken].astype(jnp.int32)


def draw_near_offset(key, part=0):
    candidates = 2 * NWIN
    numbers = jnp.arange(candidates, dtype=jnp.int32)
    first_row = jnp.arange(NCL, dtype=jnp.int32) == 0
    upper_pick = jax.random.randint(jax.random.fold_in(key, 22), (NCL,), 0, NWIN)
    lower_pick = jax.random.randint(jax.random.fold_in(key, 23), (NCL,), 0, NWIN)
    upper_pick = jnp.where(first_row, NWIN - 1, upper_pick) + NWIN
    lower_pick = jnp.where(first_row, 0, lower_pick)
    scores = jax.random.randint(jax.random.fold_in(key, 21), (NCL, candidates), 0, 2 ** 20) * candidates + numbers[None, :]
    scores = jnp.where(numbers[None, :] == upper_pick[:, None], -2, scores)
    scores = jnp.where(numbers[None, :] == lower_pick[:, None], -1, scores)
    order = jnp.argsort(scores, axis=1, stable=True)[:, :NNEAR - 1].astype(jnp.int32)
    values = order - NWIN + (order >= NWIN).astype(jnp.int32)
    first_slot = jnp.zeros((NCL, 1), jnp.int32)
    return jnp.concatenate([first_slot, values], axis=1).astype(jnp.int32)


def draw_far_offset(key, part=0):
    order = distinct_order(jax.random.fold_in(key, 31), 2 * (FWIN - NWIN), NF0)
    magnitude = NWIN + 1 + order // 2
    signs = order % 2 * 2 - 1
    return (magnitude * signs).astype(jnp.int32)


def block_scale(stream_key, extent, split, low, largest):
    def one(position, parts):
        heights = jax.random.uniform(jax.random.fold_in(jax.random.fold_in(stream_key, 6), position), (parts,), jnp.float32, low / len(split), largest / len(split))
        return jnp.repeat(jnp.exp(heights), extent[position] // parts).reshape((-1,) + (1,) * (len(extent) - position - 1))

    loudness = one(*split[0])
    for cut in split[1:]:
        loudness = loudness * one(*cut)
    return loudness


def centred(own_key, extent, width, limit, shards=(), kind=jnp.bfloat16):
    gain = block_scale(own_key, extent, shards, -0.22, 0.18) if shards else 1.0
    values = jax.random.normal(own_key, extent, jnp.float32) * width * gain
    return jnp.minimum(jnp.maximum(values, -limit), limit).astype(kind)


def setup_inputs(seed: int = 0) -> dict:
    key_of = jax.random.split(jax.random.key(seed), 14)
    potential = centred(key_of[0], (R, PANELS), 1.0, 6.0, ((0, 4), (1, 128)), jnp.float32)
    geometry = draw_geometry(jax.random.fold_in(key_of[13], 71), 0)
    near_count = draw_near_count(jax.random.fold_in(key_of[13], 71), 0)
    near_offset = draw_near_offset(jax.random.fold_in(key_of[13], 71), 0)
    far_offset = draw_far_offset(jax.random.fold_in(key_of[13], 71), 0)
    col_basis = centred(key_of[5], (NCL, P_SIZE, K), P_SIZE ** -0.5, 0.375, ((0, 128),))
    row_basis = centred(key_of[6], (NCL, P_SIZE, K), (2 * K) ** -0.5, 0.5, ((0, 128),))
    leaf_up = centred(key_of[7], (NCL, K, K), (LC_DEV * K) ** -0.5, 0.125, ((0, 128),))
    leaf_down = centred(key_of[8], (NCL, K, K), K ** -0.5, 0.75, ((0, 128),))
    leaf_coupling = centred(key_of[9], (NCL, NF0, K, K), (NF0 * K) ** -0.5, 0.375, ((0, 128),))
    up_transfer = centred(key_of[10], (2, K, K), (2 * K) ** -0.5, 0.5)
    down_transfer = centred(key_of[11], (2, K, K), K ** -0.5, 0.75)
    sibling_coupling = centred(key_of[12], (2, K, K), (4 * K) ** -0.5, 0.375)
    return dict(potential=potential, geometry=geometry, near_count=near_count, near_offset=near_offset, far_offset=far_offset, col_basis=col_basis, row_basis=row_basis, leaf_up=leaf_up, leaf_down=leaf_down, leaf_coupling=leaf_coupling, up_transfer=up_transfer, down_transfer=down_transfer, sibling_coupling=sibling_coupling)


def kernel_entries(target_geometry, source_geometry):
    squared = (target_geometry[0][:, :, None] - source_geometry[0][:, None, :]) ** 2
    squared = squared + (target_geometry[1][:, :, None] - source_geometry[1][:, None, :]) ** 2
    squared = squared + (target_geometry[2][:, :, None] - source_geometry[2][:, None, :]) ** 2
    spread = (target_geometry[3][:, :, None] + source_geometry[3][:, None, :]) / math.pi
    return source_geometry[3][:, None, :] / jnp.sqrt(squared + spread)

def reference(potential, geometry, near_count, near_offset, far_offset, col_basis, row_basis, leaf_up, leaf_down, leaf_coupling, up_transfer, down_transfer, sibling_coupling):
    all_rows = potential.shape[0]
    clusters = NCL
    rounded = potential.astype(jnp.bfloat16)
    cluster_values = rounded.reshape(all_rows, clusters, P_SIZE)
    cluster_geometry = geometry.reshape(4, clusters, P_SIZE)
    padded_values = jnp.pad(cluster_values, ((0, 0), (NWIN, NWIN), (0, 0)))
    padded_geometry = jnp.pad(cluster_geometry, ((0, 0), (NWIN, NWIN), (0, 0)))
    slot_numbers = jnp.arange(NNEAR, dtype=jnp.int32)

    def near_cluster(cluster):
        source_index = (cluster + NWIN + near_offset[cluster]).astype(jnp.int32)
        source_geometry = jnp.take(padded_geometry, source_index, axis=1)
        source_values = jnp.take(padded_values, source_index, axis=1)
        target_geometry = lax.dynamic_slice_in_dim(cluster_geometry, cluster, 1, 1)
        live_mask = (slot_numbers < near_count[cluster]).astype(jnp.float32)
        near_block = (kernel_entries(target_geometry, source_geometry) * live_mask[:, None, None]).astype(jnp.bfloat16)
        return jnp.einsum('rms,mts->rt', source_values.astype(jnp.float32), near_block.astype(jnp.float32), precision=lax.Precision.HIGHEST)
    near_field = lax.map(near_cluster, jnp.arange(clusters, dtype=jnp.int32))
    near_field = jnp.transpose(near_field, (1, 0, 2)).reshape(all_rows, clusters * P_SIZE)
    coefficients = jnp.einsum('rcp,cpk->rck', cluster_values.astype(jnp.float32), col_basis.astype(jnp.float32), precision=lax.Precision.HIGHEST).astype(jnp.bfloat16)
    padded_coefs = jnp.pad(coefficients, ((0, 0), (FWIN, FWIN), (0, 0)))
    partner_index = (jnp.arange(clusters, dtype=jnp.int32)[:, None] + FWIN + far_offset).astype(jnp.int32)
    partners = jnp.take(padded_coefs, partner_index.reshape(-1), axis=1).reshape(all_rows, clusters, NF0, K)
    leaf_far = jnp.einsum('rcmk,cmkj->rcj', partners.astype(jnp.float32), leaf_coupling.astype(jnp.float32), precision=lax.Precision.HIGHEST)
    tree_layer = jnp.einsum('rdlk,dlkj->drj', coefficients.reshape(all_rows, N_LEAF, LC_DEV, K).astype(jnp.float32), leaf_up.reshape(N_LEAF, LC_DEV, K, K).astype(jnp.float32), precision=lax.Precision.HIGHEST).astype(jnp.bfloat16)
    couplings = []
    for tree_level in range(LEVELS):
        node_count = tree_layer.shape[0]
        paired = tree_layer.reshape(node_count // 2, 2, all_rows, K).astype(jnp.float32)
        to_left = jnp.einsum('grk,kj->grj', paired[:, 1], sibling_coupling[0].astype(jnp.float32), precision=lax.Precision.HIGHEST)
        to_right = jnp.einsum('grk,kj->grj', paired[:, 0], sibling_coupling[1].astype(jnp.float32), precision=lax.Precision.HIGHEST)
        couplings.append(jnp.stack([to_left, to_right], axis=1).reshape(node_count, all_rows, K))
        if tree_level + 1 < LEVELS:
            upward = jnp.einsum('grk,kj->grj', paired[:, 0], up_transfer[0].astype(jnp.float32), precision=lax.Precision.HIGHEST)
            upward = upward + jnp.einsum('grk,kj->grj', paired[:, 1], up_transfer[1].astype(jnp.float32), precision=lax.Precision.HIGHEST)
            tree_layer = upward.astype(jnp.bfloat16)
    local_sum = jnp.zeros((1, all_rows, K), jnp.float32)
    for tree_level in reversed(range(LEVELS)):
        node_count = couplings[tree_level].shape[0]
        repeated = jnp.repeat(local_sum, 2, axis=0)
        step_down = down_transfer.astype(jnp.float32)[jnp.arange(node_count, dtype=jnp.int32) % 2]
        local_sum = couplings[tree_level] + jnp.einsum('grk,gkj->grj', repeated, step_down, precision=lax.Precision.HIGHEST)
    per_leaf = jnp.repeat(local_sum, LC_DEV, axis=0)
    leaf_local = leaf_far + jnp.einsum('crk,ckj->rcj', per_leaf, leaf_down.astype(jnp.float32), precision=lax.Precision.HIGHEST)
    leaf_local = leaf_local.astype(jnp.bfloat16)
    far_field = jnp.einsum('rck,cpk->rcp', leaf_local.astype(jnp.float32), row_basis.astype(jnp.float32), precision=lax.Precision.HIGHEST)
    return near_field + far_field.reshape(all_rows, clusters * P_SIZE)
```

```python
import math

import jax
import jax.numpy as jnp
from jax import lax
from jax.experimental import pallas as pl
from jax.experimental.pallas import tpu as pltpu
from jax.sharding import PartitionSpec as P

NWIN = 6
FWIN = 8
LANES = 256
F32 = jnp.float32
BF16 = jnp.bfloat16
NT = (((1,), (1,)), ((), ()))


def whole(shape):
    return pl.BlockSpec(shape, lambda *_: (0,) * len(shape))


def mm(left, right):
    return jnp.dot(left, right, preferred_element_type=F32)


def mm_nt(left, right):
    return lax.dot_general(left, right, NT, preferred_element_type=F32)


def span(cluster):
    start = cluster * LANES
    if not isinstance(start, int):
        start = pl.multiple_of(start, LANES)
    return pl.ds(start, LANES)


def pieces(value):
    high = value.astype(BF16)
    rest = value - high.astype(F32)
    middle = rest.astype(BF16)
    low = (rest - middle.astype(F32)).astype(BF16)
    return high, middle, low


def column(row):
    halves = [
        jnp.broadcast_to(row[:, at : at + 128], (128, 128)).T for at in range(0, LANES, 128)
    ]
    return jnp.concatenate(halves, axis=0)


def inverse_distance(columns, rows):
    parts = []
    for at in range(0, LANES, 128):
        row = rows[:, at : at + 128]
        dx = columns[0] - row[0:1]
        dy = columns[1] - row[1:2]
        dz = columns[2] - row[2:3]
        squared = dx * dx + dy * dy + dz * dz + (columns[3] + row[3:4])
        parts.append(lax.rsqrt(squared).astype(BF16))
    return jnp.concatenate(parts, axis=1)


def masked(values, bits, place):
    return (values.astype(F32) * ((bits >> place) & 1).astype(F32)).astype(BF16)


def halo_message(dens_edge, geo_edge, coefs):
    edge = NWIN * LANES
    split = [piece.astype(F32) for piece in pieces(geo_edge)]
    split = jnp.concatenate(split + [jnp.zeros((4, edge), F32)], axis=0)
    wide = FWIN * 64
    coef_rows = jnp.concatenate(coefs, axis=1)
    below = jnp.concatenate([split, jnp.zeros((16, wide), F32)], axis=1).astype(BF16)
    above = jnp.concatenate([dens_edge, coef_rows], axis=1)
    return jnp.concatenate([above, below], axis=0)


def first_kernel(
    pot, geo, count, offset, basis, up, dens, scaled, coef, top, down_msg, up_msg, bits, total
):
    step = pl.program_id(0)
    steps = pl.num_programs(0)
    per_step = basis.shape[0]
    geometry = jnp.concatenate([geo[0:3, :], geo[3:4, :] * (1.0 / math.pi)], axis=0)
    scaled[...] = geometry
    coefs = []
    raised = None
    for local in range(per_step):
        rounded = pot[:, span(local)].astype(BF16)
        dens[:, span(local)] = (rounded.astype(F32) * geo[3:4, span(local)]).astype(BF16)
        value = mm_nt(rounded, basis[local]).astype(BF16)
        coef[local] = value
        coefs.append(value)
        product = mm(value, up[local])
        raised = product if raised is None else raised + product

    @pl.when(step == 0)
    def _():
        total[...] = raised
        slots = lax.broadcasted_iota(jnp.int32, offset.shape, 0)
        live = jnp.where(slots < count[...], jnp.left_shift(1, offset[...] + NWIN), 0)
        bits[...] = jnp.sum(live, axis=0, keepdims=True)
        edge = NWIN * LANES
        down_msg[...] = halo_message(dens[:, :edge], geometry[:, :edge], coefs)

    @pl.when(step > 0)
    def _():
        total[...] += raised

    @pl.when(step == steps - 1)
    def _():
        edge = (per_step - NWIN) * LANES
        up_msg[...] = halo_message(dens[:, edge:], geometry[:, edge:], coefs)
        packed = total[...]
        packed = jnp.concatenate([packed[:16], packed[16:]], axis=1).astype(BF16)
        for peer in range(top.shape[0]):
            top[peer] = packed


def near_kernel(first, last, bits, dens, geo, *refs):
    start, (out, held_a, held_b) = refs[:-3], refs[-3:]
    clusters = dens.shape[1] // LANES

    def prepare(cluster, held):
        rows = geo[:, span(jnp.minimum(cluster, clusters - 1))]
        for k in range(4):
            held[k] = column(rows[k : k + 1])

    def sweep(cluster, held, ahead):
        columns = [held.at[k][...] for k in range(4)]
        own = dens[:, span(cluster)]
        total = None
        for d in range(ahead):
            block = inverse_distance(columns, geo[:, span(cluster + d)])
            if d == 0:
                total = mm_nt(own, block)
                continue
            source = masked(dens[:, span(cluster + d)], bits[0, cluster], NWIN + d)
            total = total + mm_nt(source, block)
            back = masked(own, bits[0, cluster + d], NWIN - d)
            out[:, span(cluster + d)] += mm(back, block)
        out[:, span(cluster)] += total

    if first == 0:
        out[...] = jnp.zeros_like(out)
    else:
        out[...] = start[0][...]
    prepare(first, held_a)

    def pair(index, carry):
        cluster = first + index * 2
        prepare(cluster + 1, held_b)
        sweep(cluster, held_a, NWIN + 1)
        prepare(cluster + 2, held_a)
        sweep(cluster + 1, held_b, NWIN + 1)
        return carry

    full = (min(last, clusters - NWIN) - first) // 2
    lax.fori_loop(0, full, pair, 0)
    for cluster in range(first + full * 2, last):
        now, later = (held_a, held_b) if (cluster - first) % 2 == 0 else (held_b, held_a)
        if cluster + 1 < last:
            prepare(cluster + 1, later)
        sweep(cluster, now, min(NWIN + 1, clusters - cluster))


def side_by_side(one):
    zero = jnp.zeros((64, 64), BF16)
    return jnp.concatenate(
        [jnp.concatenate([one, zero], axis=1), jnp.concatenate([zero, one], axis=1)], axis=0
    )


def climb(current, up, place, nodes, top):
    sides = [side_by_side(up[side]) for side in range(2)]
    levels = (current.shape[0] // 16).bit_length() - 1
    siblings = []
    for level in range(levels):
        count = current.shape[0] // 16
        nodes[0 : count * 16] = current
        other = (place >> level) ^ 1
        siblings.append(nodes[pl.ds(pl.multiple_of(other * 16, 16), 16), :])
        if top or level + 1 < levels:
            paired = current.reshape(count // 2, 2, 16, 128)
            left = paired[:, 0].reshape(count * 8, 128)
            right = paired[:, 1].reshape(count * 8, 128)
            current = (mm(left, sides[0]) + mm(right, sides[1])).astype(BF16)
    return jnp.concatenate(siblings, axis=1), current


def middle_kernel(place, tops, up, siblings, spread, nodes):
    group = tops.shape[0] // 16
    siblings[...], root = climb(tops[...], up, place[0] & (group - 1), nodes, True)
    for peer in range(spread.shape[0]):
        spread[peer] = root


def last_kernel(
    bits,
    far,
    place,
    near,
    dens,
    geo,
    below,
    above,
    low_siblings,
    tops,
    coef,
    coupling,
    leaf_down,
    basis,
    up,
    down,
    sibling,
    out,
    window,
    weights_high,
    weights_low,
    nodes,
):
    clusters = coef.shape[0]
    levels = weights_high.shape[0] // 128
    device = place[0]
    edge = NWIN * LANES

    for j in range(FWIN):
        lanes = slice(edge + j * 64, edge + (j + 1) * 64)
        window[j] = below[0:32, lanes]
        window[FWIN + clusters + j] = above[0:32, lanes]
    window[FWIN : FWIN + clusters] = coef[...]

    weights_high[...] = jnp.zeros_like(weights_high)
    weights_low[...] = jnp.zeros_like(weights_low)
    path = None
    for level in range(levels):
        side = (device >> level) & 1
        coupled = sibling[side]
        if path is None:
            weight = coupled.astype(F32)
            path = down[side].astype(F32)
        else:
            high, middle, low = pieces(path)
            weight = mm(coupled, high) + mm(coupled, middle) + mm(coupled, low)
            step_down = down[side]
            path = mm(step_down, high) + mm(step_down, middle) + mm(step_down, low)
        high, middle, _ = pieces(weight)
        for at in (0, 64):
            rows = slice(level * 128 + at, level * 128 + at + 64)
            weights_high[rows, at : at + 64] = high
            weights_low[rows, at : at + 64] = middle

    below_levels = low_siblings.shape[1] // 128
    high_siblings, _ = climb(tops[...], up, device >> below_levels, nodes, False)
    stacked = jnp.concatenate([low_siblings[...], high_siblings], axis=1)
    packed = mm(stacked, weights_high[...]) + mm(stacked, weights_low[...])
    local = jnp.concatenate([packed[:, :64], packed[:, 64:]], axis=0)
    local_high, local_low, _ = pieces(local)

    outer = [msg[32:48, :edge].astype(F32) for msg in (below, above)]
    outer = [part[0:4] + part[4:8] + part[8:12] for part in outer]
    for i in range(NWIN):
        for target, msg, geometry, sources in (
            (i, below, outer[0], range(i, NWIN)),
            (clusters - NWIN + i, above, outer[1], range(i + 1)),
        ):
            rows = geo[:, span(target)]
            columns = [column(rows[k : k + 1]) for k in range(4)]
            total = near[:, span(target)]
            for j in sources:
                apart = (j - NWIN if msg is below else clusters + j) - target
                lanes = slice(j * LANES, (j + 1) * LANES)
                block = inverse_distance(columns, geometry[:, lanes])
                source = masked(msg[0:32, lanes], bits[0, target], NWIN + apart)
                total = total + mm_nt(source, block)
            out[:, span(target)] = total
    for cluster in range(NWIN, clusters - NWIN):
        out[:, span(cluster)] = near[:, span(cluster)]

    unroll = 4

    def group(index, carry):
        for k in range(unroll):
            cluster = index * unroll + k
            partners = [window[cluster + FWIN + far[m, cluster]] for m in range(4)]
            partners = jnp.concatenate(partners, axis=1)
            total = mm(partners, coupling[cluster])
            step_down = leaf_down[cluster]
            total = total + (mm(local_high, step_down) + mm(local_low, step_down))
            out[:, span(cluster)] += mm(total.astype(BF16), basis[cluster])
        return carry

    lax.fori_loop(0, clusters // unroll, group, 0)


def per_device(
    potential,
    geometry,
    near_count,
    near_offset,
    far_offset,
    col_basis,
    row_basis,
    leaf_up,
    leaf_down,
    leaf_coupling,
    up_transfer,
    down_transfer,
    sibling_coupling,
):
    rows, width = potential.shape
    clusters, panels, rank = col_basis.shape
    per_step = FWIN
    params = pltpu.CompilerParams(vmem_limit_bytes=56 * 2**20)
    shape = jax.ShapeDtypeStruct
    lanes = per_step * panels
    message = (48, NWIN * panels + FWIN * rank)
    devices = lax.axis_size("leaf")
    levels = devices.bit_length() - 1
    outer = 2 ** (levels // 2)
    inner = devices // outer
    dens, scaled, coef, top, down_msg, up_msg, bits = pl.pallas_call(
        first_kernel,
        grid=(clusters // per_step,),
        in_specs=[
            pl.BlockSpec((rows, lanes), lambda i: (0, i)),
            pl.BlockSpec((4, lanes), lambda i: (0, i)),
            whole((1, clusters)),
            whole((near_offset.shape[1], clusters)),
            pl.BlockSpec((per_step, rank, panels), lambda i: (i, 0, 0)),
            pl.BlockSpec((per_step, rank, rank), lambda i: (i, 0, 0)),
        ],
        out_specs=[
            pl.BlockSpec((rows, lanes), lambda i: (0, i)),
            pl.BlockSpec((4, lanes), lambda i: (0, i)),
            pl.BlockSpec((per_step, rows, rank), lambda i: (i, 0, 0)),
            whole((inner, 16, 128)),
            whole(message),
            whole(message),
            whole((1, clusters)),
        ],
        out_shape=[
            shape((rows, width), BF16),
            shape((4, width), F32),
            shape((clusters, rows, rank), BF16),
            shape((inner, 16, 128), BF16),
            shape(message, BF16),
            shape(message, BF16),
            shape((1, clusters), jnp.int32),
        ],
        scratch_shapes=[pltpu.VMEM((rows, rank), F32)],
        compiler_params=params,
        name="first",
    )(
        potential,
        geometry,
        near_count.reshape(1, clusters),
        near_offset.T,
        col_basis.transpose(0, 2, 1),
        leaf_up,
    )
    upward = [(i, i + 1) for i in range(devices - 1)]
    downward = [(j, i) for i, j in upward]
    near_groups = [[at * inner + i for i in range(inner)] for at in range(outer)]
    far_groups = [[at * inner + i for at in range(outer)] for i in range(inner)]
    place = lax.axis_index("leaf").reshape(1).astype(jnp.int32)
    tops = lax.all_to_all(top, "leaf", 0, 0, axis_index_groups=near_groups)
    below = lax.ppermute(up_msg, "leaf", upward)
    above = lax.ppermute(down_msg, "leaf", downward)

    def near_part(first, last, *start):
        operands = (dens, scaled, *start)
        return pl.pallas_call(
            lambda *refs: near_kernel(first, last, *refs),
            grid_spec=pltpu.PrefetchScalarGridSpec(
                num_scalar_prefetch=1,
                grid=(1,),
                in_specs=[whole(x.shape) for x in operands],
                out_specs=whole((rows, width)),
                scratch_shapes=[pltpu.VMEM((4, panels, 128), F32)] * 2,
            ),
            out_shape=shape((rows, width), F32),
            compiler_params=params,
            cost_estimate=pl.CostEstimate(
                flops=(last - first) * 10**9 // 2,
                transcendentals=(last - first) * 7 * 65536,
                bytes_accessed=2 * 10**6,
            ),
            name="near",
        )(bits, *operands)

    cut = 12
    near = near_part(0, cut)
    tops, near = lax.optimization_barrier((tops, near))
    low_siblings, spread = pl.pallas_call(
        middle_kernel,
        grid_spec=pltpu.PrefetchScalarGridSpec(
            num_scalar_prefetch=1,
            grid=(1,),
            in_specs=[whole((inner * 16, 128)), whole(up_transfer.shape)],
            out_specs=[whole((16, (inner.bit_length() - 1) * 128)), whole((outer, 16, 128))],
            scratch_shapes=[pltpu.VMEM((inner * 16, 128), BF16)],
        ),
        out_shape=[
            shape((16, (inner.bit_length() - 1) * 128), BF16),
            shape((outer, 16, 128), BF16),
        ],
        compiler_params=params,
        name="middle",
    )(place, tops.reshape(inner * 16, 128), up_transfer)
    tops = lax.all_to_all(spread, "leaf", 0, 0, axis_index_groups=far_groups)
    near = near_part(cut, clusters, near, low_siblings)
    operands = (
        near,
        dens,
        scaled,
        below,
        above,
        low_siblings,
        tops.reshape(outer * 16, 128),
        coef,
        leaf_coupling.reshape(clusters, 4 * rank, rank),
        leaf_down,
        row_basis.transpose(0, 2, 1),
        up_transfer,
        down_transfer,
        sibling_coupling,
    )
    return pl.pallas_call(
        last_kernel,
        grid_spec=pltpu.PrefetchScalarGridSpec(
            num_scalar_prefetch=3,
            grid=(1,),
            in_specs=[whole(x.shape) for x in operands],
            out_specs=whole((rows, width)),
            scratch_shapes=[
                pltpu.VMEM((clusters + 2 * FWIN, rows, rank), BF16),
                pltpu.VMEM((levels * 128, 128), BF16),
                pltpu.VMEM((levels * 128, 128), BF16),
                pltpu.VMEM((outer * 16, 128), BF16),
            ],
        ),
        out_shape=shape((rows, width), F32),
        compiler_params=params,
        name="last",
    )(bits, far_offset.T, place, *operands)


def solution(mesh):
    placed = (
        P("rhs", "leaf"),
        P(None, "leaf"),
        P("leaf"),
        P("leaf", None),
        P("leaf", None),
        P("leaf", None, None),
        P("leaf", None, None),
        P("leaf", None, None),
        P("leaf", None, None),
        P("leaf", None, None, None),
        P(),
        P(),
        P(),
    )
    return jax.shard_map(
        per_device, mesh=mesh, in_specs=placed, out_specs=P("rhs", "leaf"), check_vma=False
    )
```

```python
import math

import jax
import jax.numpy as jnp
from jax import lax
from jax.experimental import pallas as pl
from jax.experimental.pallas import tpu as pltpu
from jax.sharding import PartitionSpec as P

NWIN = 6
FWIN = 8
LANES = 256
F32 = jnp.float32
BF16 = jnp.bfloat16
NT = (((1,), (1,)), ((), ()))


def whole(shape):
    return pl.BlockSpec(shape, lambda *_: (0,) * len(shape))


def mm(left, right):
    return jnp.dot(left, right, preferred_element_type=F32)


def mm_nt(left, right):
    return lax.dot_general(left, right, NT, preferred_element_type=F32)


def span(cluster):
    start = cluster * LANES
    if not isinstance(start, int):
        start = pl.multiple_of(start, LANES)
    return pl.ds(start, LANES)


def pieces(value):
    high = value.astype(BF16)
    rest = value - high.astype(F32)
    middle = rest.astype(BF16)
    low = (rest - middle.astype(F32)).astype(BF16)
    return high, middle, low


def column(row):
    halves = [
        jnp.broadcast_to(row[:, at : at + 128], (128, 128)).T for at in range(0, LANES, 128)
    ]
    return jnp.concatenate(halves, axis=0)


def inverse_distance(held, spread, rows):
    parts = []
    for at in range(0, LANES, 128):
        row = rows[:, at : at + 128]
        dx = (held[0] - row[0:1]).astype(BF16)
        dy = (held[1] - row[1:2]).astype(BF16)
        dz = (held[2] - row[2:3]).astype(BF16)
        squared = (dx * dx + dy * dy) + (dz * dz + (spread[...] + row[3:4].astype(BF16)))
        parts.append(lax.rsqrt(squared))
    return jnp.concatenate(parts, axis=1)


def masked(values, bits, place):
    return values * ((bits >> place) & 1).astype(F32).astype(BF16)


def halo_message(dens_edge, geo_edge, coefs):
    edge = NWIN * LANES
    split = [piece.astype(F32) for piece in pieces(geo_edge)]
    split = jnp.concatenate(split + [jnp.zeros((4, edge), F32)], axis=0)
    wide = FWIN * 64
    coef_rows = jnp.concatenate(coefs, axis=1)
    below = jnp.concatenate([split, jnp.zeros((16, wide), F32)], axis=1).astype(BF16)
    above = jnp.concatenate([dens_edge, coef_rows], axis=1)
    return jnp.concatenate([above, below], axis=0)


def first_kernel(
    pot, geo, count, offset, basis, up, dens, scaled, coef, top, down_msg, up_msg, bits, total
):
    step = pl.program_id(0)
    steps = pl.num_programs(0)
    per_step = basis.shape[0]
    geometry = jnp.concatenate([geo[0:3, :], geo[3:4, :] * (1.0 / math.pi)], axis=0)
    scaled[...] = geometry
    coefs = []
    raised = None
    for local in range(per_step):
        rounded = pot[:, span(local)].astype(BF16)
        dens[:, span(local)] = (rounded.astype(F32) * geo[3:4, span(local)]).astype(BF16)
        value = mm_nt(rounded, basis[local]).astype(BF16)
        coef[local] = value
        coefs.append(value)
        product = mm(value, up[local])
        raised = product if raised is None else raised + product

    @pl.when(step == 0)
    def _():
        total[...] = raised
        slots = lax.broadcasted_iota(jnp.int32, offset.shape, 0)
        live = jnp.where(slots < count[...], jnp.left_shift(1, offset[...] + NWIN), 0)
        bits[...] = jnp.sum(live, axis=0, keepdims=True)
        edge = NWIN * LANES
        down_msg[...] = halo_message(dens[:, :edge], geometry[:, :edge], coefs)

    @pl.when(step > 0)
    def _():
        total[...] += raised

    @pl.when(step == steps - 1)
    def _():
        edge = (per_step - NWIN) * LANES
        up_msg[...] = halo_message(dens[:, edge:], geometry[:, edge:], coefs)
        packed = total[...]
        packed = jnp.concatenate([packed[:16], packed[16:]], axis=1).astype(BF16)
        for peer in range(top.shape[0]):
            top[peer] = packed


class Sweep:
    def __init__(self, bits, dens, geo, out, held):
        self.bits, self.dens, self.geo, self.out, self.held = bits, dens, geo, out, held
        self.clusters = dens.shape[1] // LANES
        self.turn = 0

    def prepare(self, cluster):
        held, spread = self.held[self.turn % 2]
        self.turn += 1
        rows = self.geo[:, span(cluster)]
        for k in range(3):
            held[k] = column(rows[k : k + 1])
        spread[...] = column(rows[3:4]).astype(BF16)
        return held, spread

    def run(self, cluster, ready, apart, outer):
        own = self.dens[:, span(cluster)]
        mine = self.bits[0, cluster]
        total = None
        for d in apart:
            other = cluster + d
            inside = 0 <= other < self.clusters
            if inside:
                rows, source = self.geo[:, span(other)], self.dens[:, span(other)]
            else:
                rows, source = outer(other)
            block = inverse_distance(*ready, rows)
            if d:
                source = masked(source, mine, NWIN + d)
            part = mm_nt(source, block)
            total = part if total is None else total + part
            if inside and d:
                back = masked(own, self.bits[0, other], NWIN - d)
                self.out[:, span(other)] += mm(back, block)
        self.out[:, span(cluster)] += total

    def all(self, jobs, beside=lambda index: None, outer=None):
        ready = self.prepare(jobs[0][0])
        for index, (cluster, apart) in enumerate(jobs):
            now = ready
            if index + 1 < len(jobs):
                ready = self.prepare(jobs[index + 1][0])
            self.run(cluster, now, apart, outer)
            beside(index)


def near_kernel(last, bits, dens, geo, out, held_a, held_b, spread_a, spread_b):
    out[...] = jnp.zeros_like(out)
    sweep = Sweep(bits, dens, geo, out, ((held_a, spread_a), (held_b, spread_b)))
    sweep.all([(cluster, range(NWIN + 1)) for cluster in range(last)])


def edge_kernel(
    first,
    bits,
    far,
    place,
    dens,
    geo,
    start,
    below,
    above,
    coef,
    coupling,
    down,
    sibling,
    after,
    out,
    leaf_far,
    weights_high,
    weights_low,
    held_a,
    held_b,
    spread_a,
    spread_b,
    window,
    loaded,
    arrived,
):
    clusters = coef.shape[0]
    copy = pltpu.make_async_copy(coupling, loaded, arrived)
    copy.start()
    levels = weights_high.shape[0] // 128
    edge = NWIN * LANES
    out[...] = start[...]
    weights_high[...] = jnp.zeros_like(weights_high)
    weights_low[...] = jnp.zeros_like(weights_low)

    for j in range(FWIN):
        lanes = slice(edge + j * 64, edge + (j + 1) * 64)
        window[j] = below[0:32, lanes]
        window[FWIN + clusters + j] = above[0:32, lanes]
    window[FWIN : FWIN + clusters] = coef[...]

    messages = []
    for message in (below, above):
        parts = message[32:48, :edge].astype(F32)
        messages.append((message, parts[0:4] + parts[4:8] + parts[8:12]))

    def outer(cluster):
        which, at = (0, cluster + NWIN) if cluster < 0 else (1, cluster - clusters)
        message, geometry = messages[which]
        lanes = slice(at * LANES, (at + 1) * LANES)
        return geometry[:, lanes], message[0:32, lanes]

    jobs = [(cluster, range(NWIN + 1)) for cluster in range(first, clusters)]
    jobs += [(cluster, range(-NWIN, -cluster)) for cluster in range(NWIN)]
    share = -(-clusters // (len(jobs) - 1))
    path = [None]

    def beside(index):
        if index == 0:
            copy.wait()
            return
        for cluster in range((index - 1) * share, min(clusters, index * share)):
            partners = [window[cluster + FWIN + far[m, cluster]] for m in range(4)]
            leaf_far[cluster] = mm(jnp.concatenate(partners, axis=1), loaded[cluster])
        level = index - 1
        if level < levels:
            side = (place[0] >> level) & 1
            coupled = sibling[side]
            step_down = down[side]
            if level == 0:
                weight = coupled.astype(F32)
                path[0] = step_down.astype(F32)
            else:
                high, middle, low = pieces(path[0])
                weight = mm(coupled, high) + mm(coupled, middle) + mm(coupled, low)
                path[0] = mm(step_down, high) + mm(step_down, middle) + mm(step_down, low)
            high, middle, _ = pieces(weight)
            for at in (0, 64):
                rows = slice(level * 128 + at, level * 128 + at + 64)
                weights_high[rows, at : at + 64] = high
                weights_low[rows, at : at + 64] = middle

    sweep = Sweep(bits, dens, geo, out, ((held_a, spread_a), (held_b, spread_b)))
    sweep.all(jobs, beside, outer)


def side_by_side(one):
    zero = jnp.zeros((64, 64), BF16)
    return jnp.concatenate(
        [jnp.concatenate([one, zero], axis=1), jnp.concatenate([zero, one], axis=1)], axis=0
    )


def climb(current, up, place, nodes, top):
    sides = [side_by_side(up[side]) for side in range(2)]
    levels = (current.shape[0] // 16).bit_length() - 1
    siblings = []
    base = 0
    for level in range(levels):
        count = current.shape[0] // 16
        nodes[base : base + count * 16] = current
        other = (place >> level) ^ 1
        siblings.append(nodes[pl.ds(pl.multiple_of(base + other * 16, 16), 16), :])
        base += count * 16
        if top or level + 1 < levels:
            paired = current.reshape(count // 2, 2, 16, 128)
            left = paired[:, 0].reshape(count * 8, 128)
            right = paired[:, 1].reshape(count * 8, 128)
            current = (mm(left, sides[0]) + mm(right, sides[1])).astype(BF16)
    return jnp.concatenate(siblings, axis=1), current


def middle_kernel(place, tops, up, siblings, spread, nodes):
    group = tops.shape[0] // 16
    siblings[...], root = climb(tops[...], up, place[0] & (group - 1), nodes, True)
    for peer in range(spread.shape[0]):
        spread[peer] = root


def last_kernel(
    place,
    low_siblings,
    tops,
    up,
    weights_high,
    weights_low,
    near,
    leaf_far,
    leaf_down,
    basis,
    out,
    nodes,
    local,
):
    @pl.when(pl.program_id(0) == 0)
    def _():
        below_levels = low_siblings.shape[1] // 128
        high_siblings, _ = climb(tops[...], up, place[0] >> below_levels, nodes, False)
        stacked = jnp.concatenate([low_siblings[...], high_siblings], axis=1)
        packed = mm(stacked, weights_high[...]) + mm(stacked, weights_low[...])
        value = jnp.concatenate([packed[:, :64], packed[:, 64:]], axis=0)
        local[0], local[1], _ = pieces(value)

    high, low = local[0], local[1]
    for cluster in range(basis.shape[0]):
        step_down = leaf_down[cluster]
        total = leaf_far[cluster] + (mm(high, step_down) + mm(low, step_down))
        lanes = span(cluster)
        out[:, lanes] = near[:, lanes] + mm(total.astype(BF16), basis[cluster])


def per_device(
    potential,
    geometry,
    near_count,
    near_offset,
    far_offset,
    col_basis,
    row_basis,
    leaf_up,
    leaf_down,
    leaf_coupling,
    up_transfer,
    down_transfer,
    sibling_coupling,
):
    rows, width = potential.shape
    clusters, panels, rank = col_basis.shape
    per_step = FWIN
    params = pltpu.CompilerParams(vmem_limit_bytes=56 * 2**20)
    shape = jax.ShapeDtypeStruct
    lanes = per_step * panels
    message = (48, NWIN * panels + FWIN * rank)
    devices = lax.axis_size("leaf")
    levels = devices.bit_length() - 1
    outer = 2 ** (levels // 2)
    inner = devices // outer
    dens, scaled, coef, top, down_msg, up_msg, bits = pl.pallas_call(
        first_kernel,
        grid=(clusters // per_step,),
        in_specs=[
            pl.BlockSpec((rows, lanes), lambda i: (0, i)),
            pl.BlockSpec((4, lanes), lambda i: (0, i)),
            whole((1, clusters)),
            whole((near_offset.shape[1], clusters)),
            pl.BlockSpec((per_step, rank, panels), lambda i: (i, 0, 0)),
            pl.BlockSpec((per_step, rank, rank), lambda i: (i, 0, 0)),
        ],
        out_specs=[
            pl.BlockSpec((rows, lanes), lambda i: (0, i)),
            pl.BlockSpec((4, lanes), lambda i: (0, i)),
            pl.BlockSpec((per_step, rows, rank), lambda i: (i, 0, 0)),
            whole((inner, 16, 128)),
            whole(message),
            whole(message),
            whole((1, clusters)),
        ],
        out_shape=[
            shape((rows, width), BF16),
            shape((4, width), F32),
            shape((clusters, rows, rank), BF16),
            shape((inner, 16, 128), BF16),
            shape(message, BF16),
            shape(message, BF16),
            shape((1, clusters), jnp.int32),
        ],
        scratch_shapes=[pltpu.VMEM((rows, rank), F32)],
        compiler_params=params,
        name="first",
    )(
        potential,
        geometry,
        near_count.reshape(1, clusters),
        near_offset.T,
        col_basis.transpose(0, 2, 1),
        leaf_up,
    )
    upward = [(i, i + 1) for i in range(devices - 1)]
    downward = [(j, i) for i, j in upward]
    near_groups = [[at * inner + i for i in range(inner)] for at in range(outer)]
    far_groups = [[at * inner + i for at in range(outer)] for i in range(inner)]
    place = lax.axis_index("leaf").reshape(1).astype(jnp.int32)
    tops = lax.all_to_all(top, "leaf", 0, 0, axis_index_groups=near_groups)
    below = lax.ppermute(up_msg, "leaf", upward)
    above = lax.ppermute(down_msg, "leaf", downward)

    columns = [pltpu.VMEM((3, panels, 128), F32)] * 2 + [pltpu.VMEM((panels, 128), BF16)] * 2
    cut = 12
    near = pl.pallas_call(
        lambda *refs: near_kernel(cut, *refs),
        grid_spec=pltpu.PrefetchScalarGridSpec(
            num_scalar_prefetch=1,
            grid=(1,),
            in_specs=[whole((rows, width)), whole((4, width))],
            out_specs=whole((rows, width)),
            scratch_shapes=columns,
        ),
        out_shape=shape((rows, width), F32),
        compiler_params=params,
        cost_estimate=pl.CostEstimate(
            flops=6 * 10**9, transcendentals=84 * 65536, bytes_accessed=2 * 10**6
        ),
        name="near",
    )(bits, dens, scaled)
    tops, near = lax.optimization_barrier((tops, near))
    low_siblings, spread = pl.pallas_call(
        middle_kernel,
        grid_spec=pltpu.PrefetchScalarGridSpec(
            num_scalar_prefetch=1,
            grid=(1,),
            in_specs=[whole((inner * 16, 128)), whole(up_transfer.shape)],
            out_specs=[whole((16, (inner.bit_length() - 1) * 128)), whole((outer, 16, 128))],
            scratch_shapes=[pltpu.VMEM((inner * 32, 128), BF16)],
        ),
        out_shape=[
            shape((16, (inner.bit_length() - 1) * 128), BF16),
            shape((outer, 16, 128), BF16),
        ],
        compiler_params=params,
        name="middle",
    )(place, tops.reshape(inner * 16, 128), up_transfer)
    tops = lax.all_to_all(spread, "leaf", 0, 0, axis_index_groups=far_groups)
    operands = (
        dens,
        scaled,
        near,
        below,
        above,
        coef,
        leaf_coupling.reshape(clusters, 4 * rank, rank),
        down_transfer,
        sibling_coupling,
        low_siblings,
    )
    specs = [whole(x.shape) for x in operands]
    specs[6] = pl.BlockSpec(memory_space=pl.ANY)
    weights = (levels * 128, 128)
    near, leaf_far, weights_high, weights_low = pl.pallas_call(
        lambda *refs: edge_kernel(cut, *refs),
        grid_spec=pltpu.PrefetchScalarGridSpec(
            num_scalar_prefetch=3,
            grid=(1,),
            in_specs=specs,
            out_specs=[
                whole((rows, width)),
                whole((clusters, rows, rank)),
                whole(weights),
                whole(weights),
            ],
            scratch_shapes=columns
            + [
                pltpu.VMEM((clusters + 2 * FWIN, rows, rank), BF16),
                pltpu.VMEM((clusters, 4 * rank, rank), BF16),
                pltpu.SemaphoreType.DMA,
            ],
        ),
        out_shape=[
            shape((rows, width), F32),
            shape((clusters, rows, rank), F32),
            shape(weights, BF16),
            shape(weights, BF16),
        ],
        compiler_params=params,
        cost_estimate=pl.CostEstimate(
            flops=12 * 10**9, transcendentals=161 * 65536, bytes_accessed=4 * 10**6
        ),
        name="edge",
    )(bits, far_offset.T, place, *operands)

    def chunk(tail):
        return pl.BlockSpec((per_step,) + tail, lambda i, *_: (i,) + (0,) * len(tail))

    strip = pl.BlockSpec((rows, lanes), lambda i, *_: (0, i))
    return pl.pallas_call(
        last_kernel,
        grid_spec=pltpu.PrefetchScalarGridSpec(
            num_scalar_prefetch=1,
            grid=(clusters // per_step,),
            in_specs=[
                whole(low_siblings.shape),
                whole((outer * 16, 128)),
                whole(up_transfer.shape),
                whole(weights),
                whole(weights),
                strip,
                chunk((rows, rank)),
                chunk((rank, rank)),
                chunk((rank, panels)),
            ],
            out_specs=strip,
            scratch_shapes=[
                pltpu.VMEM((outer * 32, 128), BF16),
                pltpu.VMEM((2, rows, rank), BF16),
            ],
        ),
        out_shape=shape((rows, width), F32),
        compiler_params=params,
        name="last",
    )(
        place,
        low_siblings,
        tops.reshape(outer * 16, 128),
        up_transfer,
        weights_high,
        weights_low,
        near,
        leaf_far,
        leaf_down,
        row_basis.transpose(0, 2, 1),
    )


def solution(mesh):
    placed = (
        P("rhs", "leaf"),
        P(None, "leaf"),
        P("leaf"),
        P("leaf", None),
        P("leaf", None),
        P("leaf", None, None),
        P("leaf", None, None),
        P("leaf", None, None),
        P("leaf", None, None),
        P("leaf", None, None, None),
        P(),
        P(),
        P(),
    )
    return jax.shard_map(
        per_device, mesh=mesh, in_specs=placed, out_specs=P("rhs", "leaf"), check_vma=False
    )
```

```python
import math

import jax
import jax.numpy as jnp
from jax import lax
from jax.experimental import pallas as pl
from jax.experimental.pallas import tpu as pltpu
from jax.sharding import PartitionSpec as P

NWIN = 6
FWIN = 8
LANES = 256
F32 = jnp.float32
BF16 = jnp.bfloat16
NT = (((1,), (1,)), ((), ()))


def keep(value):
    return pltpu.with_memory_space_constraint(value, pltpu.VMEM)


def whole(shape):
    return pl.BlockSpec(shape, lambda *_: (0,) * len(shape))


def mm(left, right):
    return jnp.dot(left, right, preferred_element_type=F32)


def mm_nt(left, right):
    return lax.dot_general(left, right, NT, preferred_element_type=F32)


def span(cluster):
    start = cluster * LANES
    if not isinstance(start, int):
        start = pl.multiple_of(start, LANES)
    return pl.ds(start, LANES)


def pieces(value):
    high = value.astype(BF16)
    rest = value - high.astype(F32)
    middle = rest.astype(BF16)
    low = (rest - middle.astype(F32)).astype(BF16)
    return high, middle, low


def column(row):
    halves = [
        jnp.broadcast_to(row[:, at : at + 128], (128, 128)).T for at in range(0, LANES, 128)
    ]
    return jnp.concatenate(halves, axis=0)


def inverse_distance(held, spread, rows):
    parts = []
    for at in range(0, LANES, 128):
        row = rows[:, at : at + 128]
        dx = (held[0] - row[0:1]).astype(BF16)
        dy = (held[1] - row[1:2]).astype(BF16)
        dz = (held[2] - row[2:3]).astype(BF16)
        squared = (dx * dx + dy * dy) + (dz * dz + (spread[...] + row[3:4].astype(BF16)))
        parts.append(lax.rsqrt(squared))
    return jnp.concatenate(parts, axis=1)


def masked(values, bits, place):
    return values * ((bits >> place) & 1).astype(F32).astype(BF16)


def halo_message(dens_edge, geo_edge, coefs):
    edge = NWIN * LANES
    split = [piece.astype(F32) for piece in pieces(geo_edge)]
    split = jnp.concatenate(split + [jnp.zeros((4, edge), F32)], axis=0)
    wide = FWIN * 64
    coef_rows = jnp.concatenate(coefs, axis=1)
    below = jnp.concatenate([split, jnp.zeros((16, wide), F32)], axis=1).astype(BF16)
    above = jnp.concatenate([dens_edge, coef_rows], axis=1)
    return jnp.concatenate([above, below], axis=0)


def first_kernel(
    pot, geo, count, offset, basis, up, dens, scaled, coef, top, down_msg, up_msg, bits, total
):
    step = pl.program_id(0)
    steps = pl.num_programs(0)
    per_step = basis.shape[0]
    geometry = jnp.concatenate([geo[0:3, :], geo[3:4, :] * (1.0 / math.pi)], axis=0)
    scaled[...] = geometry
    coefs = []
    raised = None
    for local in range(per_step):
        rounded = pot[:, span(local)].astype(BF16)
        dens[:, span(local)] = (rounded.astype(F32) * geo[3:4, span(local)]).astype(BF16)
        value = mm_nt(rounded, basis[local]).astype(BF16)
        coef[local] = value
        coefs.append(value)
        product = mm(value, up[local])
        raised = product if raised is None else raised + product

    @pl.when(step == 0)
    def _():
        total[...] = raised
        slots = lax.broadcasted_iota(jnp.int32, offset.shape, 0)
        live = jnp.where(slots < count[...], jnp.left_shift(1, offset[...] + NWIN), 0)
        bits[...] = jnp.sum(live, axis=0, keepdims=True)
        edge = NWIN * LANES
        down_msg[...] = halo_message(dens[:, :edge], geometry[:, :edge], coefs)

    @pl.when(step > 0)
    def _():
        total[...] += raised

    @pl.when(step == steps - 1)
    def _():
        edge = (per_step - NWIN) * LANES
        up_msg[...] = halo_message(dens[:, edge:], geometry[:, edge:], coefs)
        packed = total[...]
        packed = jnp.concatenate([packed[:16], packed[16:]], axis=1).astype(BF16)
        for peer in range(top.shape[0]):
            top[peer] = packed


class Sweep:
    def __init__(self, bits, dens, geo, out, held):
        self.bits, self.dens, self.geo, self.out, self.held = bits, dens, geo, out, held
        self.clusters = dens.shape[1] // LANES
        self.turn = 0

    def prepare(self, cluster):
        held, spread = self.held[self.turn % 2]
        self.turn += 1
        rows = self.geo[:, span(cluster)]
        for k in range(3):
            held[k] = column(rows[k : k + 1])
        spread[...] = column(rows[3:4]).astype(BF16)
        return held, spread

    def run(self, cluster, ready, apart, outer):
        own = self.dens[:, span(cluster)]
        mine = self.bits[0, cluster]
        total = None
        for d in apart:
            other = cluster + d
            inside = 0 <= other < self.clusters
            if inside:
                rows, source = self.geo[:, span(other)], self.dens[:, span(other)]
            else:
                rows, source = outer(other)
            block = inverse_distance(*ready, rows)
            if d:
                source = masked(source, mine, NWIN + d)
            part = mm_nt(source, block)
            total = part if total is None else total + part
            if inside and d:
                back = masked(own, self.bits[0, other], NWIN - d)
                self.out[:, span(other)] += mm(back, block)
        self.out[:, span(cluster)] += total

    def all(self, jobs, beside=lambda index: None, outer=None):
        ready = self.prepare(jobs[0][0])
        for index, (cluster, apart) in enumerate(jobs):
            now = ready
            if index + 1 < len(jobs):
                ready = self.prepare(jobs[index + 1][0])
            self.run(cluster, now, apart, outer)
            beside(index)


def near_kernel(last, bits, dens, geo, out, held_a, held_b, spread_a, spread_b):
    out[...] = jnp.zeros_like(out)
    sweep = Sweep(bits, dens, geo, out, ((held_a, spread_a), (held_b, spread_b)))
    sweep.all([(cluster, range(NWIN + 1)) for cluster in range(last)])


def edge_kernel(
    first,
    bits,
    far,
    place,
    dens,
    geo,
    start,
    below,
    above,
    coef,
    coupling,
    down,
    sibling,
    after,
    out,
    leaf_far,
    weights_high,
    weights_low,
    held_a,
    held_b,
    spread_a,
    spread_b,
    window,
    loaded,
    arrived,
):
    clusters = coef.shape[0]
    copy = pltpu.make_async_copy(coupling, loaded, arrived)
    copy.start()
    levels = weights_high.shape[0] // 128
    edge = NWIN * LANES
    out[...] = start[...]
    weights_high[...] = jnp.zeros_like(weights_high)
    weights_low[...] = jnp.zeros_like(weights_low)

    for j in range(FWIN):
        lanes = slice(edge + j * 64, edge + (j + 1) * 64)
        window[j] = below[0:32, lanes]
        window[FWIN + clusters + j] = above[0:32, lanes]
    window[FWIN : FWIN + clusters] = coef[...]

    messages = []
    for message in (below, above):
        parts = message[32:48, :edge].astype(F32)
        messages.append((message, parts[0:4] + parts[4:8] + parts[8:12]))

    def outer(cluster):
        which, at = (0, cluster + NWIN) if cluster < 0 else (1, cluster - clusters)
        message, geometry = messages[which]
        lanes = slice(at * LANES, (at + 1) * LANES)
        return geometry[:, lanes], message[0:32, lanes]

    jobs = [(cluster, range(NWIN + 1)) for cluster in range(first, clusters)]
    jobs += [(cluster, range(-NWIN, -cluster)) for cluster in range(NWIN)]
    share = -(-clusters // (len(jobs) - 1))
    path = [None]

    def beside(index):
        if index == 0:
            copy.wait()
            return
        for cluster in range((index - 1) * share, min(clusters, index * share)):
            partners = [window[cluster + FWIN + far[m, cluster]] for m in range(4)]
            leaf_far[cluster] = mm(jnp.concatenate(partners, axis=1), loaded[cluster])
        level = index - 1
        if level < levels:
            side = (place[0] >> level) & 1
            coupled = sibling[side]
            step_down = down[side]
            if level == 0:
                weight = coupled.astype(F32)
                path[0] = step_down.astype(F32)
            else:
                high, middle, low = pieces(path[0])
                weight = mm(coupled, high) + mm(coupled, middle) + mm(coupled, low)
                path[0] = mm(step_down, high) + mm(step_down, middle) + mm(step_down, low)
            high, middle, _ = pieces(weight)
            for at in (0, 64):
                rows = slice(level * 128 + at, level * 128 + at + 64)
                weights_high[rows, at : at + 64] = high
                weights_low[rows, at : at + 64] = middle

    sweep = Sweep(bits, dens, geo, out, ((held_a, spread_a), (held_b, spread_b)))
    sweep.all(jobs, beside, outer)


def side_by_side(one):
    zero = jnp.zeros((64, 64), BF16)
    return jnp.concatenate(
        [jnp.concatenate([one, zero], axis=1), jnp.concatenate([zero, one], axis=1)], axis=0
    )


def climb(current, up, place, nodes, top):
    sides = [side_by_side(up[side]) for side in range(2)]
    levels = (current.shape[0] // 16).bit_length() - 1
    siblings = []
    base = 0
    for level in range(levels):
        count = current.shape[0] // 16
        nodes[base : base + count * 16] = current
        other = (place >> level) ^ 1
        siblings.append(nodes[pl.ds(pl.multiple_of(base + other * 16, 16), 16), :])
        base += count * 16
        if top or level + 1 < levels:
            paired = current.reshape(count // 2, 2, 16, 128)
            left = paired[:, 0].reshape(count * 8, 128)
            right = paired[:, 1].reshape(count * 8, 128)
            current = (mm(left, sides[0]) + mm(right, sides[1])).astype(BF16)
    return jnp.concatenate(siblings, axis=1), current


def middle_kernel(place, tops, up, siblings, spread, nodes):
    group = tops.shape[0] // 16
    siblings[...], root = climb(tops[...], up, place[0] & (group - 1), nodes, True)
    for peer in range(spread.shape[0]):
        spread[peer] = root


def last_kernel(
    place,
    low_siblings,
    tops,
    up,
    weights_high,
    weights_low,
    near,
    leaf_far,
    leaf_down,
    basis,
    out,
    nodes,
    local,
):
    @pl.when(pl.program_id(0) == 0)
    def _():
        below_levels = low_siblings.shape[1] // 128
        high_siblings, _ = climb(tops[...], up, place[0] >> below_levels, nodes, False)
        stacked = jnp.concatenate([low_siblings[...], high_siblings], axis=1)
        packed = mm(stacked, weights_high[...]) + mm(stacked, weights_low[...])
        value = jnp.concatenate([packed[:, :64], packed[:, 64:]], axis=0)
        local[0], local[1], _ = pieces(value)

    high, low = local[0], local[1]
    for cluster in range(basis.shape[0]):
        step_down = leaf_down[cluster]
        total = leaf_far[cluster] + (mm(high, step_down) + mm(low, step_down))
        lanes = span(cluster)
        out[:, lanes] = near[:, lanes] + mm(total.astype(BF16), basis[cluster])


def per_device(
    potential,
    geometry,
    near_count,
    near_offset,
    far_offset,
    col_basis,
    row_basis,
    leaf_up,
    leaf_down,
    leaf_coupling,
    up_transfer,
    down_transfer,
    sibling_coupling,
):
    rows, width = potential.shape
    clusters, panels, rank = col_basis.shape
    per_step = FWIN
    params = pltpu.CompilerParams(vmem_limit_bytes=56 * 2**20)
    shape = jax.ShapeDtypeStruct
    lanes = per_step * panels
    message = (48, NWIN * panels + FWIN * rank)
    devices = lax.axis_size("leaf")
    levels = devices.bit_length() - 1
    outer = 2 ** (levels // 2)
    inner = devices // outer
    dens, scaled, coef, top, down_msg, up_msg, bits = pl.pallas_call(
        first_kernel,
        grid=(clusters // per_step,),
        in_specs=[
            pl.BlockSpec((rows, lanes), lambda i: (0, i)),
            pl.BlockSpec((4, lanes), lambda i: (0, i)),
            whole((1, clusters)),
            whole((near_offset.shape[1], clusters)),
            pl.BlockSpec((per_step, rank, panels), lambda i: (i, 0, 0)),
            pl.BlockSpec((per_step, rank, rank), lambda i: (i, 0, 0)),
        ],
        out_specs=[
            pl.BlockSpec((rows, lanes), lambda i: (0, i)),
            pl.BlockSpec((4, lanes), lambda i: (0, i)),
            pl.BlockSpec((per_step, rows, rank), lambda i: (i, 0, 0)),
            whole((inner, 16, 128)),
            whole(message),
            whole(message),
            whole((1, clusters)),
        ],
        out_shape=[
            shape((rows, width), BF16),
            shape((4, width), F32),
            shape((clusters, rows, rank), BF16),
            shape((inner, 16, 128), BF16),
            shape(message, BF16),
            shape(message, BF16),
            shape((1, clusters), jnp.int32),
        ],
        scratch_shapes=[pltpu.VMEM((rows, rank), F32)],
        compiler_params=params,
        name="first",
    )(
        potential,
        geometry,
        near_count.reshape(1, clusters),
        near_offset.T,
        col_basis.transpose(0, 2, 1),
        leaf_up,
    )
    upward = [(i, i + 1) for i in range(devices - 1)]
    downward = [(j, i) for i, j in upward]
    near_groups = [[at * inner + i for i in range(inner)] for at in range(outer)]
    far_groups = [[at * inner + i for at in range(outer)] for i in range(inner)]
    place = lax.axis_index("leaf").reshape(1).astype(jnp.int32)
    tops = lax.all_to_all(top, "leaf", 0, 0, axis_index_groups=near_groups)
    below = lax.ppermute(up_msg, "leaf", upward)
    above = lax.ppermute(down_msg, "leaf", downward)

    columns = [pltpu.VMEM((3, panels, 128), F32)] * 2 + [pltpu.VMEM((panels, 128), BF16)] * 2
    cut = 12
    near = pl.pallas_call(
        lambda *refs: near_kernel(cut, *refs),
        grid_spec=pltpu.PrefetchScalarGridSpec(
            num_scalar_prefetch=1,
            grid=(1,),
            in_specs=[whole((rows, width)), whole((4, width))],
            out_specs=whole((rows, width)),
            scratch_shapes=columns,
        ),
        out_shape=shape((rows, width), F32),
        compiler_params=params,
        cost_estimate=pl.CostEstimate(
            flops=6 * 10**9, transcendentals=84 * 65536, bytes_accessed=2 * 10**6
        ),
        name="near",
    )(bits, dens, scaled)
    tops, near = lax.optimization_barrier((tops, near))
    low_siblings, spread = pl.pallas_call(
        middle_kernel,
        grid_spec=pltpu.PrefetchScalarGridSpec(
            num_scalar_prefetch=1,
            in_specs=[pl.BlockSpec(memory_space=pltpu.VMEM), whole(up_transfer.shape)],
            out_specs=[whole((16, (inner.bit_length() - 1) * 128)), whole((outer, 16, 128))],
            scratch_shapes=[pltpu.VMEM((inner * 32, 128), BF16)],
        ),
        out_shape=[
            shape((16, (inner.bit_length() - 1) * 128), BF16),
            shape((outer, 16, 128), BF16),
        ],
        compiler_params=params,
        name="middle",
    )(place, keep(tops.reshape(inner * 16, 128)), up_transfer)
    tops = lax.all_to_all(spread, "leaf", 0, 0, axis_index_groups=far_groups)
    operands = (
        dens,
        scaled,
        near,
        keep(below),
        keep(above),
        coef,
        leaf_coupling.reshape(clusters, 4 * rank, rank),
        down_transfer,
        sibling_coupling,
        low_siblings,
    )
    specs = [whole(x.shape) for x in operands]
    specs[6] = pl.BlockSpec(memory_space=pl.ANY)
    specs[3] = specs[4] = pl.BlockSpec(memory_space=pltpu.VMEM)
    weights = (levels * 128, 128)
    near, leaf_far, weights_high, weights_low = pl.pallas_call(
        lambda *refs: edge_kernel(cut, *refs),
        grid_spec=pltpu.PrefetchScalarGridSpec(
            num_scalar_prefetch=3,
            grid=(1,),
            in_specs=specs,
            out_specs=[
                whole((rows, width)),
                whole((clusters, rows, rank)),
                whole(weights),
                whole(weights),
            ],
            scratch_shapes=columns
            + [
                pltpu.VMEM((clusters + 2 * FWIN, rows, rank), BF16),
                pltpu.VMEM((clusters, 4 * rank, rank), BF16),
                pltpu.SemaphoreType.DMA,
            ],
        ),
        out_shape=[
            shape((rows, width), F32),
            shape((clusters, rows, rank), F32),
            shape(weights, BF16),
            shape(weights, BF16),
        ],
        compiler_params=params,
        cost_estimate=pl.CostEstimate(
            flops=12 * 10**9, transcendentals=161 * 65536, bytes_accessed=4 * 10**6
        ),
        name="edge",
    )(bits, far_offset.T, place, *operands)

    def chunk(tail):
        return pl.BlockSpec((per_step,) + tail, lambda i, *_: (i,) + (0,) * len(tail))

    strip = pl.BlockSpec((rows, lanes), lambda i, *_: (0, i))
    return pl.pallas_call(
        last_kernel,
        grid_spec=pltpu.PrefetchScalarGridSpec(
            num_scalar_prefetch=1,
            grid=(clusters // per_step,),
            in_specs=[
                whole(low_siblings.shape),
                pl.BlockSpec(memory_space=pltpu.VMEM),
                whole(up_transfer.shape),
                whole(weights),
                whole(weights),
                strip,
                chunk((rows, rank)),
                chunk((rank, rank)),
                chunk((rank, panels)),
            ],
            out_specs=strip,
            scratch_shapes=[
                pltpu.VMEM((outer * 32, 128), BF16),
                pltpu.VMEM((2, rows, rank), BF16),
            ],
        ),
        out_shape=shape((rows, width), F32),
        compiler_params=params,
        name="last",
    )(
        place,
        low_siblings,
        keep(tops.reshape(outer * 16, 128)),
        up_transfer,
        weights_high,
        weights_low,
        near,
        leaf_far,
        leaf_down,
        row_basis.transpose(0, 2, 1),
    )


def solution(mesh):
    placed = (
        P("rhs", "leaf"),
        P(None, "leaf"),
        P("leaf"),
        P("leaf", None),
        P("leaf", None),
        P("leaf", None, None),
        P("leaf", None, None),
        P("leaf", None, None),
        P("leaf", None, None),
        P("leaf", None, None, None),
        P(),
        P(),
        P(),
    )
    return jax.shard_map(
        per_device, mesh=mesh, in_specs=placed, out_specs=P("rhs", "leaf"), check_vma=False
    )
```

```python
import math

import jax
import jax.numpy as jnp
from jax import lax
from jax.experimental import pallas as pl
from jax.experimental.pallas import tpu as pltpu
from jax.sharding import PartitionSpec as P

NWIN = 6
FWIN = 8
LANES = 256
F32 = jnp.float32
BF16 = jnp.bfloat16
NT = (((1,), (1,)), ((), ()))


def keep(value):
    return pltpu.with_memory_space_constraint(value, pltpu.VMEM)


def whole(shape):
    return pl.BlockSpec(shape, lambda *_: (0,) * len(shape))


def mm(left, right):
    return jnp.dot(left, right, preferred_element_type=F32)


def mm_nt(left, right):
    return lax.dot_general(left, right, NT, preferred_element_type=F32)


def span(cluster):
    start = cluster * LANES
    if not isinstance(start, int):
        start = pl.multiple_of(start, LANES)
    return pl.ds(start, LANES)


def pieces(value):
    high = value.astype(BF16)
    rest = value - high.astype(F32)
    middle = rest.astype(BF16)
    low = (rest - middle.astype(F32)).astype(BF16)
    return high, middle, low


def column(row):
    halves = [
        jnp.broadcast_to(row[:, at : at + 128], (128, 128)).T for at in range(0, LANES, 128)
    ]
    return jnp.concatenate(halves, axis=0)


def inverse_distance(held, spread, rows):
    parts = []
    for at in range(0, LANES, 128):
        row = rows[:, at : at + 128]
        dx = (held[0] - row[0:1]).astype(BF16)
        dy = (held[1] - row[1:2]).astype(BF16)
        dz = (held[2] - row[2:3]).astype(BF16)
        squared = (dx * dx + dy * dy) + (dz * dz + (spread[...] + row[3:4].astype(BF16)))
        parts.append(lax.rsqrt(squared))
    return jnp.concatenate(parts, axis=1)


def masked(values, bits, place):
    return values * ((bits >> place) & 1).astype(F32).astype(BF16)


def halo_message(dens_edge, geo_edge, coefs):
    edge = NWIN * LANES
    split = [piece.astype(F32) for piece in pieces(geo_edge)]
    split = jnp.concatenate(split + [jnp.zeros((4, edge), F32)], axis=0)
    wide = FWIN * 64
    coef_rows = jnp.concatenate(coefs, axis=1)
    below = jnp.concatenate([split, jnp.zeros((16, wide), F32)], axis=1).astype(BF16)
    above = jnp.concatenate([dens_edge, coef_rows], axis=1)
    return jnp.concatenate([above, below], axis=0)


def first_kernel(
    pot, geo, count, offset, basis, up, dens, scaled, coef, top, down_msg, up_msg, bits, total
):
    step = pl.program_id(0)
    steps = pl.num_programs(0)
    per_step = basis.shape[0]
    geometry = jnp.concatenate([geo[0:3, :], geo[3:4, :] * (1.0 / math.pi)], axis=0)
    scaled[...] = geometry
    coefs = []
    raised = None
    for local in range(per_step):
        rounded = pot[:, span(local)].astype(BF16)
        dens[:, span(local)] = (rounded.astype(F32) * geo[3:4, span(local)]).astype(BF16)
        value = mm_nt(rounded, basis[local]).astype(BF16)
        coef[local] = value
        coefs.append(value)
        product = mm(value, up[local])
        raised = product if raised is None else raised + product

    @pl.when(step == 0)
    def _():
        total[...] = raised
        slots = lax.broadcasted_iota(jnp.int32, offset.shape, 0)
        live = jnp.where(slots < count[...], jnp.left_shift(1, offset[...] + NWIN), 0)
        bits[...] = jnp.sum(live, axis=0, keepdims=True)
        edge = NWIN * LANES
        down_msg[...] = halo_message(dens[:, :edge], geometry[:, :edge], coefs)

    @pl.when(step > 0)
    def _():
        total[...] += raised

    @pl.when(step == steps - 1)
    def _():
        edge = (per_step - NWIN) * LANES
        up_msg[...] = halo_message(dens[:, edge:], geometry[:, edge:], coefs)
        packed = total[...]
        packed = jnp.concatenate([packed[:16], packed[16:]], axis=1).astype(BF16)
        for peer in range(top.shape[0]):
            top[peer] = packed


class Sweep:
    def __init__(self, bits, dens, geo, out, held):
        self.bits, self.dens, self.geo, self.out, self.held = bits, dens, geo, out, held
        self.clusters = dens.shape[1] // LANES
        self.turn = 0

    def prepare(self, cluster):
        held, spread = self.held[self.turn % 2]
        self.turn += 1
        rows = self.geo[:, span(cluster)]
        for k in range(3):
            held[k] = column(rows[k : k + 1])
        spread[...] = column(rows[3:4]).astype(BF16)
        return held, spread

    def run(self, cluster, ready, apart, outer):
        own = self.dens[:, span(cluster)]
        mine = self.bits[0, cluster]
        total = None
        for d in apart:
            other = cluster + d
            inside = 0 <= other < self.clusters
            if inside:
                rows, source = self.geo[:, span(other)], self.dens[:, span(other)]
            else:
                rows, source = outer(other)
            block = inverse_distance(*ready, rows)
            if d:
                source = masked(source, mine, NWIN + d)
            part = mm_nt(source, block)
            total = part if total is None else total + part
            if inside and d:
                back = masked(own, self.bits[0, other], NWIN - d)
                self.out[:, span(other)] += mm(back, block)
        self.out[:, span(cluster)] += total

    def all(self, jobs, beside=lambda index: None, outer=None):
        ready = self.prepare(jobs[0][0])
        for index, (cluster, apart) in enumerate(jobs):
            now = ready
            if index + 1 < len(jobs):
                ready = self.prepare(jobs[index + 1][0])
            self.run(cluster, now, apart, outer)
            beside(index)


def near_kernel(last, bits, dens, geo, out, held_a, held_b, spread_a, spread_b):
    out[...] = jnp.zeros_like(out)
    sweep = Sweep(bits, dens, geo, out, ((held_a, spread_a), (held_b, spread_b)))
    sweep.all([(cluster, range(NWIN + 1)) for cluster in range(last)])


def edge_kernel(
    first,
    bits,
    far,
    place,
    dens,
    geo,
    start,
    below,
    above,
    coef,
    coupling,
    down,
    sibling,
    after,
    out,
    leaf_far,
    weights_high,
    weights_low,
    held_a,
    held_b,
    spread_a,
    spread_b,
    window,
    loaded,
    arrived,
):
    clusters = coef.shape[0]
    copy = pltpu.make_async_copy(coupling, loaded, arrived)
    copy.start()
    levels = weights_high.shape[0] // 128
    edge = NWIN * LANES
    out[...] = start[...]
    weights_high[...] = jnp.zeros_like(weights_high)
    weights_low[...] = jnp.zeros_like(weights_low)

    for j in range(FWIN):
        lanes = slice(edge + j * 64, edge + (j + 1) * 64)
        window[j] = below[0:32, lanes]
        window[FWIN + clusters + j] = above[0:32, lanes]
    window[FWIN : FWIN + clusters] = coef[...]

    messages = []
    for message in (below, above):
        parts = message[32:48, :edge].astype(F32)
        messages.append((message, parts[0:4] + parts[4:8] + parts[8:12]))

    def outer(cluster):
        which, at = (0, cluster + NWIN) if cluster < 0 else (1, cluster - clusters)
        message, geometry = messages[which]
        lanes = slice(at * LANES, (at + 1) * LANES)
        return geometry[:, lanes], message[0:32, lanes]

    jobs = [(cluster, range(NWIN + 1)) for cluster in range(first, clusters)]
    jobs += [(cluster, range(-NWIN, -cluster)) for cluster in range(NWIN)]
    share = -(-clusters // (len(jobs) - 1))
    path = [None]

    def beside(index):
        if index == 0:
            copy.wait()
            return
        for cluster in range((index - 1) * share, min(clusters, index * share)):
            partners = [window[cluster + FWIN + far[m, cluster]] for m in range(4)]
            leaf_far[cluster] = mm(jnp.concatenate(partners, axis=1), loaded[cluster])
        level = index - 1
        if level < levels:
            side = (place[0] >> level) & 1
            coupled = sibling[side]
            step_down = down[side]
            if level == 0:
                weight = coupled.astype(F32)
                path[0] = step_down.astype(F32)
            else:
                high, middle, low = pieces(path[0])
                weight = mm(coupled, high) + mm(coupled, middle) + mm(coupled, low)
                path[0] = mm(step_down, high) + mm(step_down, middle) + mm(step_down, low)
            high, middle, _ = pieces(weight)
            for at in (0, 64):
                rows = slice(level * 128 + at, level * 128 + at + 64)
                weights_high[rows, at : at + 64] = high
                weights_low[rows, at : at + 64] = middle

    sweep = Sweep(bits, dens, geo, out, ((held_a, spread_a), (held_b, spread_b)))
    sweep.all(jobs, beside, outer)


def side_by_side(one):
    zero = jnp.zeros((64, 64), BF16)
    return jnp.concatenate(
        [jnp.concatenate([one, zero], axis=1), jnp.concatenate([zero, one], axis=1)], axis=0
    )


def climb(current, up, place, nodes, top):
    sides = [side_by_side(up[side]) for side in range(2)]
    levels = (current.shape[0] // 16).bit_length() - 1
    siblings = []
    base = 0
    for level in range(levels):
        count = current.shape[0] // 16
        nodes[base : base + count * 16] = current
        other = (place >> level) ^ 1
        siblings.append(nodes[pl.ds(pl.multiple_of(base + other * 16, 16), 16), :])
        base += count * 16
        if top or level + 1 < levels:
            paired = current.reshape(count // 2, 2, 16, 128)
            left = paired[:, 0].reshape(count * 8, 128)
            right = paired[:, 1].reshape(count * 8, 128)
            current = (mm(left, sides[0]) + mm(right, sides[1])).astype(BF16)
    return jnp.concatenate(siblings, axis=1), current


def middle_kernel(place, tops, up, siblings, spread, nodes):
    group = tops.shape[0] // 16
    siblings[...], root = climb(tops[...], up, place[0] & (group - 1), nodes, True)
    for peer in range(spread.shape[0]):
        spread[peer] = root


def last_kernel(
    place,
    low_siblings,
    tops,
    up,
    weights_high,
    weights_low,
    near,
    leaf_far,
    leaf_down,
    basis,
    out,
    nodes,
    local,
):
    @pl.when(pl.program_id(0) == 0)
    def _():
        below_levels = low_siblings.shape[1] // 128
        high_siblings, _ = climb(tops[...], up, place[0] >> below_levels, nodes, False)
        stacked = jnp.concatenate([low_siblings[...], high_siblings], axis=1)
        packed = mm(stacked, weights_high[...]) + mm(stacked, weights_low[...])
        value = jnp.concatenate([packed[:, :64], packed[:, 64:]], axis=0)
        local[0], local[1], _ = pieces(value)

    high, low = local[0], local[1]
    for cluster in range(basis.shape[0]):
        step_down = leaf_down[cluster]
        total = leaf_far[cluster] + (mm(high, step_down) + mm(low, step_down))
        lanes = span(cluster)
        out[:, lanes] = near[:, lanes] + mm(total.astype(BF16), basis[cluster])


def per_device(
    potential,
    geometry,
    near_count,
    near_offset,
    far_offset,
    col_basis,
    row_basis,
    leaf_up,
    leaf_down,
    leaf_coupling,
    up_transfer,
    down_transfer,
    sibling_coupling,
):
    rows, width = potential.shape
    clusters, panels, rank = col_basis.shape
    per_step = FWIN
    params = pltpu.CompilerParams(vmem_limit_bytes=56 * 2**20)
    shape = jax.ShapeDtypeStruct
    lanes = per_step * panels
    message = (48, NWIN * panels + FWIN * rank)
    devices = lax.axis_size("leaf")
    levels = devices.bit_length() - 1
    outer = 2 ** (levels // 2)
    inner = devices // outer
    dens, scaled, coef, top, down_msg, up_msg, bits = pl.pallas_call(
        first_kernel,
        grid=(clusters // per_step,),
        in_specs=[
            pl.BlockSpec((rows, lanes), lambda i: (0, i)),
            pl.BlockSpec((4, lanes), lambda i: (0, i)),
            whole((1, clusters)),
            whole((near_offset.shape[1], clusters)),
            pl.BlockSpec((per_step, rank, panels), lambda i: (i, 0, 0)),
            pl.BlockSpec((per_step, rank, rank), lambda i: (i, 0, 0)),
        ],
        out_specs=[
            pl.BlockSpec((rows, lanes), lambda i: (0, i)),
            pl.BlockSpec((4, lanes), lambda i: (0, i)),
            pl.BlockSpec((per_step, rows, rank), lambda i: (i, 0, 0)),
            whole((inner, 16, 128)),
            whole(message),
            whole(message),
            whole((1, clusters)),
        ],
        out_shape=[
            shape((rows, width), BF16),
            shape((4, width), F32),
            shape((clusters, rows, rank), BF16),
            shape((inner, 16, 128), BF16),
            shape(message, BF16),
            shape(message, BF16),
            shape((1, clusters), jnp.int32),
        ],
        scratch_shapes=[pltpu.VMEM((rows, rank), F32)],
        compiler_params=params,
        name="first",
    )(
        potential,
        geometry,
        near_count.reshape(1, clusters),
        near_offset.T,
        col_basis.transpose(0, 2, 1),
        leaf_up,
    )
    upward = [(i, i + 1) for i in range(devices - 1)]
    downward = [(j, i) for i, j in upward]
    near_groups = [[at * inner + i for i in range(inner)] for at in range(outer)]
    far_groups = [[at * inner + i for at in range(outer)] for i in range(inner)]
    place = lax.axis_index("leaf").reshape(1).astype(jnp.int32)
    tops = lax.all_to_all(top, "leaf", 0, 0, axis_index_groups=near_groups)
    below = lax.ppermute(up_msg, "leaf", upward)
    above = lax.ppermute(down_msg, "leaf", downward)

    columns = [pltpu.VMEM((3, panels, 128), F32)] * 2 + [pltpu.VMEM((panels, 128), BF16)] * 2
    cut = 12
    near = pl.pallas_call(
        lambda *refs: near_kernel(cut, *refs),
        grid_spec=pltpu.PrefetchScalarGridSpec(
            num_scalar_prefetch=1,
            grid=(1,),
            in_specs=[whole((rows, width)), whole((4, width))],
            out_specs=whole((rows, width)),
            scratch_shapes=columns,
        ),
        out_shape=shape((rows, width), F32),
        compiler_params=params,
        cost_estimate=pl.CostEstimate(
            flops=6 * 10**9, transcendentals=84 * 65536, bytes_accessed=2 * 10**6
        ),
        name="near",
    )(bits, dens, scaled)
    tops, near = lax.optimization_barrier((tops, near))
    low_siblings, spread = pl.pallas_call(
        middle_kernel,
        grid_spec=pltpu.PrefetchScalarGridSpec(
            num_scalar_prefetch=1,
            in_specs=[pl.BlockSpec(memory_space=pltpu.VMEM), whole(up_transfer.shape)],
            out_specs=[whole((16, (inner.bit_length() - 1) * 128)), whole((outer, 16, 128))],
            scratch_shapes=[pltpu.VMEM((inner * 32, 128), BF16)],
        ),
        out_shape=[
            shape((16, (inner.bit_length() - 1) * 128), BF16),
            shape((outer, 16, 128), BF16),
        ],
        compiler_params=params,
        name="middle",
    )(place, keep(tops.reshape(inner * 16, 128)), up_transfer)
    tops = lax.all_to_all(spread, "leaf", 0, 0, axis_index_groups=far_groups)
    operands = (
        dens,
        scaled,
        near,
        keep(below),
        keep(above),
        coef,
        leaf_coupling.reshape(clusters, 4 * rank, rank),
        down_transfer,
        sibling_coupling,
        low_siblings,
    )
    specs = [whole(x.shape) for x in operands]
    specs[6] = pl.BlockSpec(memory_space=pl.ANY)
    specs[3] = specs[4] = pl.BlockSpec(memory_space=pltpu.VMEM)
    weights = (levels * 128, 128)
    near, leaf_far, weights_high, weights_low = pl.pallas_call(
        lambda *refs: edge_kernel(cut, *refs),
        grid_spec=pltpu.PrefetchScalarGridSpec(
            num_scalar_prefetch=3,
            grid=(1,),
            in_specs=specs,
            out_specs=[
                whole((rows, width)),
                whole((clusters, rows, rank)),
                whole(weights),
                whole(weights),
            ],
            scratch_shapes=columns
            + [
                pltpu.VMEM((clusters + 2 * FWIN, rows, rank), BF16),
                pltpu.VMEM((clusters, 4 * rank, rank), BF16),
                pltpu.SemaphoreType.DMA,
            ],
        ),
        out_shape=[
            shape((rows, width), F32),
            shape((clusters, rows, rank), F32),
            shape(weights, BF16),
            shape(weights, BF16),
        ],
        compiler_params=params,
        cost_estimate=pl.CostEstimate(
            flops=12 * 10**9, transcendentals=161 * 65536, bytes_accessed=4 * 10**6
        ),
        name="edge",
    )(bits, far_offset.T, place, *operands)

    def chunk(tail):
        return pl.BlockSpec((2 * per_step,) + tail, lambda i, *_: (i,) + (0,) * len(tail))

    strip = pl.BlockSpec((rows, 2 * lanes), lambda i, *_: (0, i))
    return pl.pallas_call(
        last_kernel,
        grid_spec=pltpu.PrefetchScalarGridSpec(
            num_scalar_prefetch=1,
            grid=(clusters // (2 * per_step),),
            in_specs=[
                whole(low_siblings.shape),
                pl.BlockSpec(memory_space=pltpu.VMEM),
                whole(up_transfer.shape),
                whole(weights),
                whole(weights),
                strip,
                chunk((rows, rank)),
                chunk((rank, rank)),
                chunk((rank, panels)),
            ],
            out_specs=strip,
            scratch_shapes=[
                pltpu.VMEM((outer * 32, 128), BF16),
                pltpu.VMEM((2, rows, rank), BF16),
            ],
        ),
        out_shape=shape((rows, width), F32),
        compiler_params=params,
        name="last",
    )(
        place,
        low_siblings,
        keep(tops.reshape(outer * 16, 128)),
        up_transfer,
        weights_high,
        weights_low,
        near,
        leaf_far,
        leaf_down,
        row_basis.transpose(0, 2, 1),
    )


def solution(mesh):
    placed = (
        P("rhs", "leaf"),
        P(None, "leaf"),
        P("leaf"),
        P("leaf", None),
        P("leaf", None),
        P("leaf", None, None),
        P("leaf", None, None),
        P("leaf", None, None),
        P("leaf", None, None),
        P("leaf", None, None, None),
        P(),
        P(),
        P(),
    )
    return jax.shard_map(
        per_device, mesh=mesh, in_specs=placed, out_specs=P("rhs", "leaf"), check_vma=False
    )
```
